128 devices in a mesh: row: 16 (over z_lo, x, core), col: 8 (over z_hi, y).
Axes of the slice: x: 4, y: 4, z: 4 (z_hi: 2, z_lo: 2; z = z_hi * 2 + z_lo), core: 2. Of those that a mesh axis runs over, the one named last changes fastest.
Arguments:
- right_sides: bfloat16 [4, 24, 1536, 3072], P(None, None, 'row', 'col'), may hold values from -6 to 6
- to_eigen: bfloat16 [1536, 1536], replicated, may hold values from -0.15625 to 0.15625
- from_eigen: bfloat16 [1536, 1536], replicated, may hold values from -0.15625 to 0.15625
- eigenvalues: float32 [1536], replicated, may hold values from 0.05 to 20
Outputs:
- solutions: bfloat16 [4, 24, 1536, 3072], P(None, None, 'row', 'col')
The draws below stay inside these ranges and needn't reach their ends.
All inputs are finite; a program needn't handle non-finite values.
Results may differ from the reference program's by a relative error of at most 0.0049.
Values may be sent and summed in bfloat16 or wider, within the bound.
A program may use at most 192 MiB of HBM per device.

```python
import math
import jax
import jax.numpy as jnp
from jax import lax

KX = 24
KZ = 3072
NY = 1536


def level_of(rng, extent, cuts, smallest, largest):
    def one(axis_at, parts):
        steps = jax.random.uniform(jax.random.fold_in(jax.random.fold_in(rng, 6), axis_at), (parts,), jnp.float32, smallest / len(cuts), largest / len(cuts))
        return jnp.repeat(jnp.exp(steps), extent[axis_at] // parts).reshape((-1,) + (1,) * (len(extent) - axis_at - 1))

    gain = one(*cuts[0])
    for cut in cuts[1:]:
        gain = gain * one(*cut)
    return gain


def bell_draw(own_key, extent, width, limit, split=(), kind=jnp.bfloat16):
    values = width * jax.random.normal(own_key, extent, jnp.float32)
    if split:
        values = values * level_of(own_key, extent, split, -0.22, 0.18)
    return jnp.clip(values, -limit, limit).astype(kind)


def setup_inputs(seed: int = 0) -> dict:
    seeds = jax.random.split(jax.random.key(seed), 5)
    right_sides = bell_draw(seeds[0], (4, KX, NY, KZ), 1.0, 6.0, ((2, 16), (3, 8)))
    to_eigen = bell_draw(seeds[1], (NY, NY), NY ** -0.5, 0.15625)
    from_eigen = bell_draw(seeds[2], (NY, NY), NY ** -0.5, 0.15625)
    eigenvalues = jnp.clip(jnp.exp(jax.random.uniform(seeds[3], (NY,), jnp.float32, math.log(0.05), math.log(20.0))), 0.05, 20.0)
    return dict(right_sides=right_sides, to_eigen=to_eigen, from_eigen=from_eigen, eigenvalues=eigenvalues)


def reference(right_sides, to_eigen, from_eigen, eigenvalues):
    kz_values = jnp.arange(KZ, dtype=jnp.float32)
    moved = jnp.moveaxis(right_sides, 1, 0)
    kx_values = jnp.arange(KX, dtype=jnp.int32)

    def solve_wavenumber(pair):
        planes, kx_index = pair
        kx_float = kx_index.astype(jnp.float32)
        lines = jnp.transpose(planes, (1, 0, 2)).reshape(NY, 4 * KZ)
        coefficients = jnp.dot(to_eigen, lines, preferred_element_type=jnp.float32).reshape(NY, 4, KZ)
        damping = 4.0 * (kx_float ** 2 / (KX * KX) + kz_values ** 2 / (KZ * KZ))
        damping_gain = 1.0 / (1.0 + eigenvalues[:, None] + damping[None, :])
        scaled = (coefficients * damping_gain[:, None, :]).astype(jnp.bfloat16).reshape(NY, 4 * KZ)
        solved = jnp.dot(from_eigen, scaled, preferred_element_type=jnp.float32).astype(jnp.bfloat16)
        return jnp.transpose(solved.reshape(NY, 4, KZ), (1, 0, 2))

    result = lax.map(solve_wavenumber, (moved, kx_values))
    return jnp.moveaxis(result, 0, 1)
```

```python
import jax
import jax.numpy as jnp
from jax import lax
from jax.sharding import PartitionSpec as P

KX = 24
KZ = 3072


def on_device(right_sides, to_eigen, from_eigen, eigenvalues):
    comps, kx, ny_local, kz_local = right_sides.shape
    planes = comps * kx
    rows = lax.axis_size("row")
    lines = lax.all_to_all(
        right_sides.reshape(planes, ny_local, kz_local),
        "row",
        split_axis=0,
        concat_axis=1,
        tiled=True,
    )
    held = planes // rows
    plane = lax.axis_index("row") * held + jnp.arange(held, dtype=jnp.int32)
    kx_float = (plane % kx).astype(jnp.float32)
    kz_index = lax.axis_index("col") * kz_local + jnp.arange(kz_local, dtype=jnp.int32)
    kz_float = kz_index.astype(jnp.float32)
    damping = 4.0 * (kx_float[:, None] ** 2 / (KX * KX) + kz_float[None, :] ** 2 / (KZ * KZ))
    damping_gain = 1.0 / (1.0 + eigenvalues[None, :, None] + damping[:, None, :])
    coefficients = jnp.einsum("mn,gnj->gmj", to_eigen, lines, preferred_element_type=jnp.float32)
    scaled = (coefficients * damping_gain).astype(jnp.bfloat16)
    solved = jnp.einsum("mn,gnj->gmj", from_eigen, scaled, preferred_element_type=jnp.float32).astype(
        jnp.bfloat16
    )
    back = lax.all_to_all(solved, "row", split_axis=1, concat_axis=0, tiled=True)
    return back.reshape(right_sides.shape)


def solution(mesh):
    placed = (P(None, None, "row", "col"), P(), P(), P())
    return jax.shard_map(
        on_device,
        mesh=mesh,
        in_specs=placed,
        out_specs=P(None, None, "row", "col"),
        check_vma=False,
    )
```

```python
import functools

import jax
import jax.numpy as jnp
from jax import lax
from jax.experimental import pallas as pl
from jax.experimental.pallas import tpu as pltpu
from jax.sharding import PartitionSpec as P

KX = 24
KZ = 3072
MESH = pl.DeviceIdType.MESH
PAIR = 2
TILE = 256


def exchange_kernel(
    rows,
    x_ref,
    to_hbm,
    from_hbm,
    eig_ref,
    out_ref,
    lines,
    solved,
    scaled,
    to_vmem,
    from_vmem,
    weight_sem,
    own_in_sem,
    own_out_sem,
    send_in,
    recv_in,
    send_out,
    recv_out,
):
    planes, ny_local, width = x_ref.shape
    held = planes // rows
    chunks = held // PAIR
    ny = rows * ny_local
    me = lax.axis_index("row")
    col = lax.axis_index("col")
    high, middle, low = me // 8, (me // 2) % 4, me % 2

    def peer(step, sign=1):
        return (
            ((high + step // 4) % 2) * 8
            + ((middle + 4 + sign * (step % 4)) % 4) * 2
            + (low + step // 8) % 2
        )

    def rows_of(device):
        return pl.ds(pl.multiple_of(device * ny_local, ny_local), ny_local)

    def inward(k, step, j, target):
        return pltpu.make_async_remote_copy(
            src_ref=x_ref.at[target * held + k * PAIR + j],
            dst_ref=lines.at[k, rows_of(me), pl.ds(j * width, width)],
            send_sem=send_in.at[k, step, j],
            recv_sem=recv_in.at[k, step, j],
            device_id={"row": target},
            device_id_type=MESH,
        )

    def outward(k, step, j, target):
        return pltpu.make_async_remote_copy(
            src_ref=solved.at[k, rows_of(target), pl.ds(j * width, width)],
            dst_ref=out_ref.at[me * held + k * PAIR + j],
            send_sem=send_out.at[k, step, j],
            recv_sem=recv_out.at[k, step, j],
            device_id={"row": target},
            device_id_type=MESH,
        )

    def own_in(k, j):
        return pltpu.make_async_copy(
            x_ref.at[me * held + k * PAIR + j],
            lines.at[k, rows_of(me), pl.ds(j * width, width)],
            own_in_sem.at[k, j],
        )

    def own_out(k, j):
        return pltpu.make_async_copy(
            solved.at[k, rows_of(me), pl.ds(j * width, width)],
            out_ref.at[me * held + k * PAIR + j],
            own_out_sem.at[k, j],
        )

    load_to = pltpu.make_async_copy(to_hbm, to_vmem, weight_sem.at[0])
    load_from = pltpu.make_async_copy(from_hbm, from_vmem, weight_sem.at[1])

    barrier = pltpu.get_barrier_semaphore()

    @pl.loop(1, rows)
    def _(step):
        pl.semaphore_signal(barrier, inc=1, device_id={"row": peer(step)}, device_id_type=MESH)

    load_to.start()
    load_from.start()
    pl.semaphore_wait(barrier, rows - 1)

    @pl.loop(0, chunks)
    def _(k):
        @pl.loop(1, rows)
        def _(step):
            for j in range(PAIR):
                inward(k, step, j, peer(step)).start()

        for j in range(PAIR):
            own_in(k, j).start()

    load_to.wait()
    load_from.wait()

    kz = (col * width + lax.broadcasted_iota(jnp.int32, (1, width), 1)).astype(jnp.float32)

    @pl.loop(0, chunks)
    def _(k):
        for j in range(PAIR):
            own_in(k, j).wait()

        @pl.loop(1, rows)
        def _(step):
            for j in range(PAIR):
                inward(k, step, j, peer(step)).wait_recv()

        @pl.loop(0, ny // TILE)
        def _(m):
            part = pl.ds(pl.multiple_of(m * TILE, TILE), TILE)
            coefficients = jnp.dot(to_vmem[part, :], lines[k], preferred_element_type=jnp.float32)
            for j in range(PAIR):
                kx = ((me * held + k * PAIR + j) % KX).astype(jnp.float32)
                damping = 4.0 * (kx * kx / (KX * KX) + kz * kz / (KZ * KZ))
                gain = 1.0 / (1.0 + eig_ref[part, :] + damping)
                cols = slice(j * width, (j + 1) * width)
                scaled[part, cols] = (coefficients[:, cols] * gain).astype(jnp.bfloat16)

        @pl.loop(0, ny // TILE)
        def _(m):
            part = pl.ds(pl.multiple_of(m * TILE, TILE), TILE)
            solved[k, part, :] = jnp.dot(
                from_vmem[part, :], scaled[...], preferred_element_type=jnp.float32
            ).astype(jnp.bfloat16)

        @pl.loop(1, rows)
        def _(step):
            for j in range(PAIR):
                outward(k, step, j, peer(step)).start()

        for j in range(PAIR):
            own_out(k, j).start()

    @pl.loop(0, chunks)
    def _(k):
        for j in range(PAIR):
            own_out(k, j).wait()

        @pl.loop(1, rows)
        def _(step):
            for j in range(PAIR):
                inward(k, step, j, peer(step)).wait_send()
                outward(k, step, j, peer(step)).wait()


def on_device(right_sides, to_eigen, from_eigen, eigenvalues):
    comps, kx, ny_local, width = right_sides.shape
    planes = comps * kx
    rows = lax.axis_size("row")
    ny = rows * ny_local
    held = planes // rows
    chunks = held // PAIR
    anywhere = pl.BlockSpec(memory_space=pl.ANY)
    solved = pl.pallas_call(
        functools.partial(exchange_kernel, rows),
        out_shape=jax.ShapeDtypeStruct((planes, ny_local, width), jnp.bfloat16),
        in_specs=[anywhere, anywhere, anywhere, pl.BlockSpec(memory_space=pltpu.VMEM)],
        out_specs=anywhere,
        scratch_shapes=[
            pltpu.VMEM((chunks, ny, PAIR * width), jnp.bfloat16),
            pltpu.VMEM((chunks, ny, PAIR * width), jnp.bfloat16),
            pltpu.VMEM((ny, PAIR * width), jnp.bfloat16),
            pltpu.VMEM((ny, ny), jnp.bfloat16),
            pltpu.VMEM((ny, ny), jnp.bfloat16),
            pltpu.SemaphoreType.DMA((2,)),
            pltpu.SemaphoreType.DMA((chunks, PAIR)),
            pltpu.SemaphoreType.DMA((chunks, PAIR)),
            pltpu.SemaphoreType.DMA((chunks, rows, PAIR)),
            pltpu.SemaphoreType.DMA((chunks, rows, PAIR)),
            pltpu.SemaphoreType.DMA((chunks, rows, PAIR)),
            pltpu.SemaphoreType.DMA((chunks, rows, PAIR)),
        ],
        compiler_params=pltpu.CompilerParams(
            collective_id=0, has_side_effects=True, vmem_limit_bytes=48 * 2**20
        ),
    )(
        right_sides.reshape(planes, ny_local, width),
        to_eigen,
        from_eigen,
        eigenvalues.reshape(ny, 1),
    )
    return solved.reshape(right_sides.shape)


def solution(mesh):
    placed = (P(None, None, "row", "col"), P(), P(), P())
    return jax.shard_map(
        on_device,
        mesh=mesh,
        in_specs=placed,
        out_specs=P(None, None, "row", "col"),
        check_vma=False,
    )
```
